128 devices in a mesh: enc: 8 (over x, core), dp: 16 (over z, y).
Axes of the slice: x: 4, y: 4, z: 4, core: 2. Of those that a mesh axis runs over, the one named last changes fastest.
Arguments:
- patches: bfloat16 [16, 128, 64, 1280], P('dp', 'enc'), may hold values from -6 to 6
- cotangent: bfloat16 [16, 128, 64, 1280], P('dp', 'enc'), may hold values from -6 to 6
- block_dest: int32 [16, 128], P('dp', 'enc'), may hold values from -1 to 7, as said below
- window_len: int32 [16, 128], P('dp', 'enc'), may hold values from 1 to 64, as said below
- ln_gain: float32 [1280], replicated, may hold values from 0.5 to 1.5
- ln_bias: float32 [1280], replicated, may hold values from -3 to 3
- qkv_weight: bfloat16 [1280, 3840], replicated, may hold values from -4 to 4
- qkv_scale: float32 [3840], replicated, may hold values from 0.01 to 0.04
- qkv_bias: float32 [3840], replicated, may hold values from -3 to 3
- out_weight: bfloat16 [1280, 1280], replicated, may hold values from -4 to 4
- out_scale: float32 [1280], replicated, may hold values from 0.01 to 0.04
- out_bias: float32 [1280], replicated, may hold values from -3 to 3
Outputs:
- embeddings: bfloat16 [16, 128, 64, 1280], P('dp', 'enc')
- patch_grad: bfloat16 [16, 128, 64, 1280], P('dp', 'enc')
- qkv_weight_grad: float32 [1280, 3840], P(('enc', 'dp'))
- out_weight_grad: float32 [1280, 1280], P(('enc', 'dp'))
The draws below stay inside these ranges and needn't reach their ends.
Inputs may be any that keep to these rules, and one draw needn't show every extreme that they name: `block_dest`: in each data group the live blocks of each enc index come first in its 16 slots; every enc index of a group is the destination of exactly 8 blocks of that group, at most 2 from any one enc index, and some enc index sends exactly 2 to one destination; some enc index holds 16 live blocks. `window_len`: some window is full.
All inputs are finite; a program needn't handle non-finite values.
Results may differ from the reference program's by a relative error of at most 0.0098.
Values may be sent and summed in bfloat16 or wider, within the bound.
No kernel may reach another device: no remote copies, remote signals or barrier semaphores. Data moves between devices by JAX's collectives and lax.ppermute only.
A program may use at most 192 MiB of HBM per device.

```python
import math
import jax
import jax.numpy as jnp
from jax import lax

D = 1280
HEADS = 16
WIN = 64
RECV = 8
BLK_SRC = 16
MOST = 2
GROUP_BLK = 128
N_ENC = 8
N_DP = 16


def draw_block_dest(key, part):

    def one_group(group_key):
        pair_key, order_key = jax.random.split(group_key)
        spread = jax.random.randint(pair_key, (N_ENC // 2,), 0, RECV + 1)
        spread = spread.at[0].set(RECV)
        counts = jnp.stack([RECV + spread, RECV - spread], axis=1).reshape(N_ENC)
        order = jax.random.permutation(order_key, N_ENC)
        counts = counts[order]
        first = jnp.argmax(order == 0)
        sources = jnp.arange(N_ENC)
        rotated = (sources - first) % N_ENC
        before = rotated[None, :] < rotated[:, None]
        start = jnp.sum(jnp.where(before, counts[None, :], 0), axis=1)
        local = jnp.arange(BLK_SRC)
        position = start[:, None] + local[None, :]
        dest = position // MOST % N_ENC
        dest = jnp.where(local[None, :] < counts[:, None], dest, -1)
        return dest.reshape(N_ENC * BLK_SRC).astype(jnp.int32)
    group_keys = jax.random.split(jax.random.fold_in(key, 11), N_DP)
    return jax.vmap(one_group)(group_keys)


def draw_window_len(key, part):
    full_key, size_key = jax.random.split(jax.random.fold_in(key, 23))
    shape = (N_DP, N_ENC * BLK_SRC)
    is_full = jax.random.randint(full_key, shape, 0, 2)
    partial_len = jax.random.randint(size_key, shape, 1, WIN + 1)
    lengths = jnp.where(is_full == 1, WIN, partial_len)
    return lengths.at[0, 0].set(WIN).astype(jnp.int32)


def level_of(own_key, extent, shards, least, high):
    loudness, own = 1.0, jax.random.fold_in(own_key, 6)
    for dim, parts in shards:
        heights = jnp.exp(jax.random.uniform(jax.random.fold_in(own, dim), (parts,), jnp.float32, least / len(shards), high / len(shards)))
        loudness = loudness * jnp.repeat(heights, extent[dim] // parts).reshape([-1 if axis == dim else 1 for axis in range(len(extent))])
    return loudness


def bell_draw(rng, shape, scale, most, cuts=(), kind=jnp.bfloat16):
    drawn = scale * jax.random.normal(rng, shape, jnp.float32)
    if cuts:
        drawn = drawn * level_of(rng, shape, cuts, -0.22, 0.18)
    return jnp.clip(drawn, -most, most).astype(kind)


def setup_inputs(seed: int = 0) -> dict:
    streams_of = jax.random.split(jax.random.key(seed), 13)
    return {
        "patches": bell_draw(streams_of[0], (N_DP, GROUP_BLK, WIN, D), 1.0, 6.0, ((0, 16), (1, 8))),
        "cotangent": bell_draw(streams_of[1], (N_DP, GROUP_BLK, WIN, D), 1.0, 6.0, ((0, 16), (1, 8))),
        "block_dest": draw_block_dest(jax.random.fold_in(streams_of[12], 71), 0),
        "window_len": draw_window_len(jax.random.fold_in(streams_of[12], 71), 0),
        "ln_gain": jnp.clip(1.0 + 0.1 * jax.random.normal(streams_of[4], (D,), jnp.float32), 0.5, 1.5),
        "ln_bias": bell_draw(streams_of[5], (D,), 0.5, 3.0, (), jnp.float32),
        "qkv_weight": bell_draw(streams_of[6], (D, 3 * D), 1.0, 4.0),
        "qkv_scale": jnp.clip(jnp.exp(jax.random.uniform(streams_of[7], (3 * D,), jnp.float32, math.log(0.01), math.log(0.04))), 0.01, 0.04),
        "qkv_bias": bell_draw(streams_of[8], (3 * D,), 0.5, 3.0, (), jnp.float32),
        "out_weight": bell_draw(streams_of[9], (D, D), 1.0, 4.0),
        "out_scale": jnp.clip(jnp.exp(jax.random.uniform(streams_of[10], (D,), jnp.float32, math.log(0.01), math.log(0.04))), 0.01, 0.04),
        "out_bias": bell_draw(streams_of[11], (D,), 0.5, 3.0, (), jnp.float32),
    }


def contract(form, left, right):
    return jnp.einsum(form, left.astype(jnp.float32), right.astype(jnp.float32))

def window_layer(patches, lengths, cotangent, ln_gain, ln_bias, qkv_weight, qkv_scale, qkv_bias, out_weight, out_scale, out_bias, heads):
    blocks, window, width = patches.shape
    head_dim = width // heads
    scale = 1.0 / head_dim ** 0.5
    position = jnp.arange(window, dtype=jnp.int32)
    row_mask = (position[None, :] < lengths[:, None]).astype(jnp.float32)
    key_mask = (position[None, :] < jnp.maximum(lengths, 1)[:, None]).astype(jnp.float32)
    inputs = patches.astype(jnp.float32)
    centered = inputs - lax.optimization_barrier(jnp.mean(inputs, axis=-1, keepdims=True))
    inv_std = lax.rsqrt(lax.optimization_barrier(jnp.mean(centered * centered, axis=-1, keepdims=True)) + 1e-06)
    normed = centered * inv_std
    hidden = (normed * ln_gain + ln_bias).astype(jnp.bfloat16)
    flat_hidden = hidden.reshape(blocks * window, width)
    projected = jnp.dot(flat_hidden, qkv_weight, preferred_element_type=jnp.float32)
    qkv = (projected * qkv_scale + qkv_bias).astype(jnp.bfloat16).reshape(blocks, window, 3, heads, head_dim)
    query = qkv[:, :, 0]
    keys = qkv[:, :, 1]
    values = qkv[:, :, 2]
    scores = contract('bqhd,bkhd->bhqk', query, keys) * scale
    raised = jnp.exp(scores) * key_mask[:, None, None, :]
    probs = raised / lax.optimization_barrier(jnp.sum(raised, axis=-1, keepdims=True))
    probs_low = probs.astype(jnp.bfloat16)
    attended = contract('bhqk,bkhd->bqhd', probs_low, values).astype(jnp.bfloat16)
    flat_att = attended.reshape(blocks * window, width)
    output = jnp.dot(flat_att, out_weight, preferred_element_type=jnp.float32) * out_scale + out_bias
    output = output.reshape(blocks, window, width) + inputs
    embeddings = (output * row_mask[:, :, None]).astype(jnp.bfloat16)
    grad_out = cotangent.astype(jnp.float32) * row_mask[:, :, None]
    grad_scaled = (grad_out * out_scale).astype(jnp.bfloat16)
    flat_grad = grad_scaled.reshape(blocks * window, width)
    out_grad = lax.dot_general(flat_att, flat_grad, (((0,), (0,)), ((), ())), preferred_element_type=jnp.float32)
    grad_att = lax.dot_general(flat_grad, out_weight, (((1,), (1,)), ((), ())), preferred_element_type=jnp.float32)
    grad_att = grad_att.astype(jnp.bfloat16).reshape(blocks, window, heads, head_dim)
    grad_probs = contract('bqhd,bkhd->bhqk', grad_att, values)
    grad_values = contract('bhqk,bqhd->bkhd', probs_low, grad_att)
    grad_scores = probs * (grad_probs - lax.optimization_barrier(jnp.sum(probs * grad_probs, axis=-1, keepdims=True)))
    grad_low = (grad_scores * scale).astype(jnp.bfloat16)
    grad_query = contract('bhqk,bkhd->bqhd', grad_low, keys)
    grad_keys = contract('bhqk,bqhd->bkhd', grad_low, query)
    grad_qkv = jnp.stack([grad_query, grad_keys, grad_values], axis=2).reshape(blocks * window, 3 * width)
    grad_qkv = (grad_qkv * qkv_scale).astype(jnp.bfloat16)
    qkv_grad = lax.dot_general(flat_hidden, grad_qkv, (((0,), (0,)), ((), ())), preferred_element_type=jnp.float32)
    grad_hidden = lax.dot_general(grad_qkv, qkv_weight, (((1,), (1,)), ((), ())), preferred_element_type=jnp.float32)
    grad_normed = grad_hidden.reshape(blocks, window, width) * ln_gain
    grad_ln = inv_std * (grad_normed - lax.optimization_barrier(jnp.mean(grad_normed, axis=-1, keepdims=True)) - normed * lax.optimization_barrier(jnp.mean(grad_normed * normed, axis=-1, keepdims=True)))
    patch_grad = ((grad_out + grad_ln) * row_mask[:, :, None]).astype(jnp.bfloat16)
    return (embeddings, patch_grad, qkv_grad, out_grad)

def reference(patches, cotangent, block_dest, window_len, ln_gain, ln_bias, qkv_weight, qkv_scale, qkv_bias, out_weight, out_scale, out_bias):
    live_count = N_ENC * RECV

    def one_group(carry, items):
        group_x, group_dy, group_dest, group_len = items
        valid = group_dest >= 0
        chosen = jnp.nonzero(valid, size=live_count)[0].astype(jnp.int32)
        lengths = jnp.where(valid, group_len, 0).astype(jnp.int32)
        emb, pgrad, qgrad, ograd = window_layer(group_x[chosen], lengths[chosen], group_dy[chosen], ln_gain, ln_bias, qkv_weight, qkv_scale, qkv_bias, out_weight, out_scale, out_bias, HEADS)
        emb_full = jnp.zeros_like(group_x).at[chosen].set(emb)
        grad_full = jnp.zeros_like(group_x).at[chosen].set(pgrad)
        return ((carry[0] + qgrad, carry[1] + ograd), (emb_full, grad_full))
    start = (jnp.zeros((D, 3 * D), jnp.float32), jnp.zeros((D, D), jnp.float32))
    sums, outs = lax.scan(one_group, start, (patches, cotangent, block_dest, window_len))
    return (outs[0], outs[1], sums[0], sums[1])
```

```python
import jax
import jax.numpy as jnp
from jax import lax
from jax.experimental import pallas as pl
from jax.experimental.pallas import tpu as pltpu
from jax.sharding import PartitionSpec as P

D = 1280
HEADS = 16
WIN = 64
TM = 256
HALF = 640
NHP = 4
SCALE = 1.0 / 80**0.5
BF = jnp.bfloat16
F32 = jnp.float32
VMEM = 60 * 1024 * 1024


def nn(a, b):
    return lax.dot_general(a, b, (((1,), (0,)), ((), ())), preferred_element_type=F32)


def nt(a, b):
    return lax.dot_general(a, b, (((1,), (1,)), ((), ())), preferred_element_type=F32)


def lanes(shape):
    return lax.broadcasted_iota(jnp.int32, shape, 1)


def head_masks(i):
    lane = lanes((1, 256))
    lo = 32 * i
    in_a = (lane >= lo) & (lane < lo + 80)
    in_b = (lane >= lo + 80) & (lane < lo + 160)
    return in_a, in_b


def stack_heads(win, in_a, in_b):
    zero = jnp.zeros_like(win)
    return jnp.concatenate([jnp.where(in_a, win, zero), jnp.where(in_b, win, zero)], axis=0)


def pack(s):
    even = (lanes((64, 256)) // 64) % 2 == 0
    return jnp.where(even, s[:64], s[64:])


def unpack(p):
    even = (lanes((64, 256)) // 64) % 2 == 0
    zero = jnp.zeros_like(p)
    return jnp.concatenate([jnp.where(even, p, zero), jnp.where(even, zero, p)], axis=0)


def segment_ones():
    r = lax.broadcasted_iota(jnp.int32, (256, 256), 0) // 64
    c = lax.broadcasted_iota(jnp.int32, (256, 256), 1) // 64
    return jnp.where(r == c, 1.0, 0.0).astype(BF)


def segment_sum(x, ones):
    hi = x.astype(BF)
    lo = (x - hi.astype(F32)).astype(BF)
    return nn(hi, ones) + nn(lo, ones)


def pair_transpose(full):
    return jnp.concatenate([full[:, :128].T, full[:, 128:].T], axis=1)


def join_windows(w):
    tiles = [w[0][:, :128]]
    for i in range(1, NHP):
        tiles.append(w[i - 1][:, 128:] + w[i][:, :128])
    tiles.append(w[NHP - 1][:, 128:])
    return jnp.concatenate(tiles, axis=1)


def row_order(core):
    r = lax.broadcasted_iota(jnp.int32, (D, D), 0)
    c = lax.broadcasted_iota(jnp.int32, (D, D), 1)
    side = r // 640
    rest = r % 640
    d = rest // 40
    x = (rest % 40) // 10
    j = rest % 10
    e = 2 * x + jnp.bitwise_xor(core, side)
    return jnp.where(c == 160 * e + 10 * d + j, 1.0, 0.0).astype(BF)


def forward_body(
    core_ref, x_ref, dy_ref, rm_ref, km_ref, gain_ref, bias_ref, w_ref, qs_ref, qb_ref,
    os_ref, qkv_ref, p_ref, att_ref, gs_ref, ht_ref, keep_ref, send_ref,
    perm_ref, ones_ref, attt_ref, gsall_ref,
):
    step = pl.program_id(0)

    @pl.when(step == 0)
    def _():
        perm_ref[...] = row_order(core_ref[0])
        ones_ref[...] = segment_ones()

    @pl.when(step < 4)
    def _():
        x = x_ref[...].astype(F32)
        cen = x - jnp.mean(x, axis=-1, keepdims=True)
        inv = lax.rsqrt(jnp.mean(cen * cen, axis=-1, keepdims=True) + 1e-06)
        hidden = (cen * inv * gain_ref[...] + bias_ref[...]).astype(BF)
        ht_ref[...] = nt(perm_ref[...], hidden).astype(BF)
        gs = (dy_ref[...].astype(F32) * rm_ref[...] * os_ref[...]).astype(BF)
        gs_ref[...] = gs
        row = pl.multiple_of(step * TM, TM)
        gsall_ref[pl.ds(row, TM), :] = gs
        for c in range(6):
            cols = slice(c * HALF, (c + 1) * HALF)
            acc = nn(hidden, w_ref[:, cols])
            qkv_ref[:, cols] = (acc * qs_ref[:, cols] + qb_ref[:, cols]).astype(BF)
        ones = ones_ref[...]
        for b in range(2):
            rows = slice(b * 128, (b + 1) * 128)
            km = km_ref[b]
            for g in range(2):
                outs = []
                for i in range(NHP):
                    in_a, in_b = head_masks(i)
                    lo = g * HALF + 128 * i
                    q = qkv_ref[rows, lo : lo + 256]
                    k = qkv_ref[rows, D + lo : D + lo + 256]
                    v = qkv_ref[rows, 2 * D + lo : 2 * D + lo + 256]
                    s = pack(nt(q, stack_heads(k, in_a, in_b)))
                    e = jnp.exp(s * SCALE) * km
                    p = e / segment_sum(e, ones)
                    p_ref[b, g * NHP + i] = p
                    outs.append(nn(unpack(p.astype(BF)), stack_heads(v, in_a, in_b)))
                att_ref[rows, g * HALF : (g + 1) * HALF] = join_windows(outs).astype(BF)
        attt_ref[:, pl.ds(row, TM)] = nt(perm_ref[...], att_ref[...]).astype(BF)

    @pl.when((step >= 4) & (step < 6))
    def _():
        row = pl.multiple_of((step - 4) * 320, 320)
        keep_ref[...] = nn(attt_ref[pl.ds(row, 320), :], gsall_ref[...]).astype(BF)

    @pl.when(step >= 6)
    def _():
        row = pl.multiple_of((step - 4) * 320, 320)
        send_ref[...] = nn(attt_ref[pl.ds(row, 320), :], gsall_ref[...]).astype(BF)


def whole(shape):
    return pl.BlockSpec(shape, lambda i: tuple(0 for _ in shape), pipeline_mode=pl.Buffered(1))


def params():
    return pltpu.CompilerParams(
        dimension_semantics=("arbitrary",), vmem_limit_bytes=VMEM
    )


def forward_call(core, x, dy, rm, km, gain, bias, w, qs, qb, osc):
    t = x.shape[0]
    tile = lambda i: jnp.minimum(i, 3)
    rows = lambda n: pl.BlockSpec((TM, n), lambda i: (tile(i), 0))
    return pl.pallas_call(
        forward_body,
        grid=(8,),
        in_specs=[
            pl.BlockSpec(memory_space=pltpu.SMEM),
            rows(D), rows(D), rows(1),
            pl.BlockSpec((2, 1, 256), lambda i: (tile(i), 0, 0)),
            whole((1, D)), whole((1, D)), whole((D, 3 * D)),
            whole((1, 3 * D)), whole((1, 3 * D)), whole((1, D)),
        ],
        out_specs=[
            rows(3 * D),
            pl.BlockSpec((2, 8, 64, 256), lambda i: (tile(i), 0, 0, 0)),
            rows(D), rows(D),
            pl.BlockSpec((D, TM), lambda i: (0, tile(i))),
            pl.BlockSpec((320, D), lambda i: (jnp.clip(i - 4, 0, 1), 0)),
            pl.BlockSpec((320, D), lambda i: (jnp.clip(i - 6, 0, 1), 0)),
        ],
        out_shape=[
            jax.ShapeDtypeStruct((t, 3 * D), BF),
            jax.ShapeDtypeStruct((t // 128, 8, 64, 256), F32),
            jax.ShapeDtypeStruct((t, D), BF),
            jax.ShapeDtypeStruct((t, D), BF),
            jax.ShapeDtypeStruct((D, t), BF),
            jax.ShapeDtypeStruct((640, D), BF),
            jax.ShapeDtypeStruct((640, D), BF),
        ],
        scratch_shapes=[
            pltpu.VMEM((D, D), BF),
            pltpu.VMEM((256, 256), BF),
            pltpu.VMEM((D, t), BF),
            pltpu.VMEM((t, D), BF),
        ],
        compiler_params=params(),
        cost_estimate=pl.CostEstimate(
            flops=20 * 10**9, transcendentals=10**6, bytes_accessed=40 * 10**6
        ),
        name="forward",
    )(core, x, dy, rm, km, gain, bias, w, qs, qb, osc)


def backward_body(
    q_ref, k_ref, v_ref, gs_ref, wo_ref, p_ref, sq_ref, sk_ref, sv_ref, ht_ref,
    gq_ref, gk_ref, gv_ref, keep_ref, send_ref, ga_ref, all_ref, ones_ref,
):
    step = pl.program_id(0)

    @pl.when(step == 0)
    def _():
        ones_ref[...] = segment_ones()

    @pl.when(step < 4)
    def _():
        ga_ref[...] = nt(gs_ref[...], wo_ref[...]).astype(BF)
        ones = ones_ref[...]
        for b in range(2):
            rows = slice(b * 128, (b + 1) * 128)
            at = pl.multiple_of(step * TM + b * 128, 128)
            gqs, gks, gvs = [], [], []
            for i in range(NHP):
                in_a, in_b = head_masks(i)
                cols = slice(128 * i, 128 * i + 256)
                q, k, v, ga = q_ref[rows, cols], k_ref[rows, cols], v_ref[rows, cols], ga_ref[rows, cols]
                p = p_ref[b, i]
                gp = pack(nt(ga, stack_heads(v, in_a, in_b)))
                t = p * gp
                g = unpack((p * (gp - segment_sum(t, ones)) * SCALE).astype(BF))
                pf = unpack(p.astype(BF))
                gqs.append(nn(g, stack_heads(k, in_a, in_b)))
                gks.append(nn(pair_transpose(g), stack_heads(q, in_a, in_b)))
                gvs.append(nn(pair_transpose(pf), stack_heads(ga, in_a, in_b)))
            for n, (ws, s_ref, o_ref) in enumerate(
                ((gqs, sq_ref, gq_ref), (gks, sk_ref, gk_ref), (gvs, sv_ref, gv_ref))
            ):
                val = (join_windows(ws) * s_ref[...]).astype(BF)
                o_ref[rows, :] = val
                all_ref[pl.ds(at, 128), n * HALF : (n + 1) * HALF] = val

    @pl.when((step >= 4) & (step < 6))
    def _():
        row = pl.multiple_of((step - 4) * 320, 320)
        keep_ref[...] = nn(ht_ref[pl.ds(row, 320), :], all_ref[...]).astype(BF)

    @pl.when(step >= 6)
    def _():
        row = pl.multiple_of((step - 4) * 320, 320)
        send_ref[...] = nn(ht_ref[pl.ds(row, 320), :], all_ref[...]).astype(BF)


def backward_call(half, qkv, gs, wo, p, qs, ht):
    t = gs.shape[0]
    tile = lambda i: jnp.minimum(i, 3)
    third = lambda n: pl.BlockSpec((TM, HALF), lambda i: (tile(i), 2 * n + half))
    sc = lambda n: pl.BlockSpec((1, HALF), lambda i: (0, 2 * n + half))
    return pl.pallas_call(
        backward_body,
        grid=(8,),
        in_specs=[
            third(0), third(1), third(2),
            pl.BlockSpec((TM, D), lambda i: (tile(i), 0)),
            pl.BlockSpec((HALF, D), lambda i: (half, 0), pipeline_mode=pl.Buffered(1)),
            pl.BlockSpec((2, NHP, 64, 256), lambda i: (tile(i), half, 0, 0)),
            sc(0), sc(1), sc(2),
            whole((D, t)),
        ],
        out_specs=[
            pl.BlockSpec((TM, HALF), lambda i: (tile(i), 0)),
            pl.BlockSpec((TM, HALF), lambda i: (tile(i), 0)),
            pl.BlockSpec((TM, HALF), lambda i: (tile(i), 0)),
            pl.BlockSpec((320, 3 * HALF), lambda i: (jnp.clip(i - 4, 0, 1), 0)),
            pl.BlockSpec((320, 3 * HALF), lambda i: (jnp.clip(i - 6, 0, 1), 0)),
        ],
        out_shape=[jax.ShapeDtypeStruct((t, HALF), BF)] * 3
        + [jax.ShapeDtypeStruct((640, 3 * HALF), BF)] * 2,
        scratch_shapes=[
            pltpu.VMEM((TM, HALF), BF),
            pltpu.VMEM((t, 3 * HALF), BF),
            pltpu.VMEM((256, 256), BF),
        ],
        compiler_params=params(),
        cost_estimate=pl.CostEstimate(
            flops=8 * 10**9, transcendentals=0, bytes_accessed=30 * 10**6
        ),
        name="backward%d" % half,
    )(qkv, qkv, qkv, gs, wo, p, qs, qs, qs, ht)


def finish_body(
    x_ref, dy_ref, rm_ref, att_ref, g0_ref, g1_ref, g2_ref, g3_ref, g4_ref, g5_ref,
    gain_ref, w_ref, wo_ref, os_ref, ob_ref, emb_ref, pg_ref,
):
    rm = rm_ref[...]
    x = x_ref[...].astype(F32)
    out = nn(att_ref[...], wo_ref[...]) * os_ref[...] + ob_ref[...] + x
    emb_ref[...] = (out * rm).astype(BF)
    cen = x - jnp.mean(x, axis=-1, keepdims=True)
    inv = lax.rsqrt(jnp.mean(cen * cen, axis=-1, keepdims=True) + 1e-06)
    normed = cen * inv
    gh = None
    for c, r in enumerate((g0_ref, g1_ref, g2_ref, g3_ref, g4_ref, g5_ref)):
        part = nt(r[...], w_ref[:, c * HALF : (c + 1) * HALF])
        gh = part if gh is None else gh + part
    gn = gh * gain_ref[...]
    gl = inv * (
        gn
        - jnp.mean(gn, axis=-1, keepdims=True)
        - normed * jnp.mean(gn * normed, axis=-1, keepdims=True)
    )
    go = dy_ref[...].astype(F32) * rm
    pg_ref[...] = ((go + gl) * rm).astype(BF)


def finish_call(x, dy, rm, att, parts, gain, w, wo, osc, ob):
    t = x.shape[0]
    rows = lambda n: pl.BlockSpec((TM, n), lambda i: (i, 0))
    return pl.pallas_call(
        finish_body,
        grid=(t // TM,),
        in_specs=[rows(D), rows(D), rows(1), rows(D)]
        + [rows(HALF)] * 6
        + [whole((1, D)), whole((D, 3 * D)), whole((D, D)), whole((1, D)), whole((1, D))],
        out_specs=[rows(D), rows(D)],
        out_shape=[jax.ShapeDtypeStruct((t, D), BF)] * 2,
        compiler_params=params(),
        cost_estimate=pl.CostEstimate(
            flops=14 * 10**9, transcendentals=0, bytes_accessed=30 * 10**6
        ),
        name="finish",
    )(x, dy, rm, att, *parts, gain, w, wo, osc, ob)


def local_masks(dest, window_len):
    lengths = jnp.where(dest >= 0, window_len, 0)
    pos = jnp.arange(WIN, dtype=jnp.int32)
    rm = (pos[None, :] < lengths[:, None]).astype(F32).reshape(-1, 1)
    km = (pos[None, :] < jnp.maximum(lengths, 1)[:, None]).astype(F32)
    km = km.reshape(-1, 1, 128)
    return rm, jnp.concatenate([km, km], axis=2)


def reduce_piece(keep, send):
    swap = [(i, i ^ 1) for i in range(8)]
    got = lax.ppermute(send, "enc", swap)
    total = (keep + got).reshape(16, 40, -1)
    return lax.psum_scatter(total, "dp", scatter_dimension=0, tiled=True)[0]


def local_work(core, x, dy, dest, wl, gain, bias, w, qs, qb, wo, osc, ob, reduce):
    rm, km = local_masks(dest, wl)
    row = lambda a: a.reshape(1, -1)
    gain, bias, qs, qb, osc, ob = map(row, (gain, bias, qs, qb, osc, ob))
    qkv, p, att, gs, ht, okeep, osend = forward_call(
        core, x, dy, rm, km, gain, bias, w, qs, qb, osc
    )
    red_o = reduce(okeep, osend)
    gq0, gk0, gv0, keep0, send0 = backward_call(0, qkv, gs, wo, p, qs, ht)
    red_0 = reduce(keep0, send0)
    gq1, gk1, gv1, keep1, send1 = backward_call(1, qkv, gs, wo, p, qs, ht)
    red_1 = reduce(keep1, send1)
    emb, pg = finish_call(
        x, dy, rm, att, (gq0, gq1, gk0, gk1, gv0, gv1), gain, w, wo, osc, ob
    )
    return emb, pg, red_o, red_0, red_1


def per_device(x, dy, dest, wl, gain, bias, w, qs, qb, wo, osc, ob):
    core = (lax.axis_index("enc") % 2).reshape(1).astype(jnp.int32)
    shape = x.shape
    emb, pg, red_o, red_0, red_1 = local_work(
        core, x.reshape(-1, D), dy.reshape(-1, D), dest[0], wl[0],
        gain, bias, w, qs, qb, wo, osc, ob, reduce_piece,
    )
    both = jnp.concatenate([red_o, red_0, red_1], axis=1).astype(F32)
    both = both.reshape(4, 10, 4 * D)
    groups = [[0, 2, 4, 6], [1, 3, 5, 7]]
    mine = lax.psum_scatter(
        both, "enc", scatter_dimension=0, axis_index_groups=groups, tiled=True
    )[0]
    halves = mine[:, D:].reshape(10, 2, 3, HALF)
    qkv_grad = halves.transpose(0, 2, 1, 3).reshape(10, 3 * D)
    return emb.reshape(shape), pg.reshape(shape), qkv_grad, mine[:, :D]


def solution(mesh):
    big = P("dp", "enc", None, None)
    small = P("dp", "enc")
    return jax.shard_map(
        per_device,
        mesh=mesh,
        in_specs=(big, big, small, small) + (P(),) * 8,
        out_specs=(big, big, P(("enc", "dp"), None), P(("enc", "dp"), None)),
        check_vma=False,
    )
```

```python
import jax
import jax.numpy as jnp
from jax import lax
from jax.experimental import pallas as pl
from jax.experimental.pallas import tpu as pltpu
from jax.sharding import PartitionSpec as P

D = 1280
HEADS = 16
WIN = 64
TM = 256
HALF = 640
NHP = 4
SCALE = 1.0 / 80**0.5
BF = jnp.bfloat16
F32 = jnp.float32
VMEM = 60 * 1024 * 1024


def nn(a, b):
    return lax.dot_general(a, b, (((1,), (0,)), ((), ())), preferred_element_type=F32)


def nt(a, b):
    return lax.dot_general(a, b, (((1,), (1,)), ((), ())), preferred_element_type=F32)


def lanes(shape):
    return lax.broadcasted_iota(jnp.int32, shape, 1)


def head_masks(i):
    lane = lanes((1, 256))
    lo = 32 * i
    in_a = (lane >= lo) & (lane < lo + 80)
    in_b = (lane >= lo + 80) & (lane < lo + 160)
    return in_a, in_b


def stack_heads(win, in_a, in_b):
    zero = jnp.zeros_like(win)
    return jnp.concatenate([jnp.where(in_a, win, zero), jnp.where(in_b, win, zero)], axis=0)


def pack(s):
    even = (lanes((64, 256)) // 64) % 2 == 0
    return jnp.where(even, s[:64], s[64:])


def unpack(p):
    even = (lanes((64, 256)) // 64) % 2 == 0
    zero = jnp.zeros_like(p)
    return jnp.concatenate([jnp.where(even, p, zero), jnp.where(even, zero, p)], axis=0)


def segment_ones():
    r = lax.broadcasted_iota(jnp.int32, (256, 256), 0) // 64
    c = lax.broadcasted_iota(jnp.int32, (256, 256), 1) // 64
    return jnp.where(r == c, 1.0, 0.0).astype(BF)


def segment_sum(x, ones):
    hi = x.astype(BF)
    lo = (x - hi.astype(F32)).astype(BF)
    return nn(hi, ones) + nn(lo, ones)


def pair_transpose(full):
    return jnp.concatenate([full[:, :128].T, full[:, 128:].T], axis=1)


def join_windows(w):
    tiles = [w[0][:, :128]]
    for i in range(1, NHP):
        tiles.append(w[i - 1][:, 128:] + w[i][:, :128])
    tiles.append(w[NHP - 1][:, 128:])
    return jnp.concatenate(tiles, axis=1)


def row_order(index):
    core = (index // 16) % 2
    x0 = index // 32
    z0 = (index // 4) % 4
    y0 = index % 4
    r = lax.broadcasted_iota(jnp.int32, (D, 1), 0)
    c = lax.broadcasted_iota(jnp.int32, (D, D), 1)
    side = r // 640
    rest = r % 640
    z = (z0 + rest // 160) % 4
    y = (y0 + (rest % 160) // 40) % 4
    x = (x0 + (rest % 40) // 10) % 4
    e = 2 * x + jnp.bitwise_xor(core, side)
    src = 160 * e + 10 * (4 * z + y) + rest % 10
    return jnp.where(c == src, 1.0, 0.0).astype(BF)


def live_len(dest_ref, wl_ref, b):
    return jnp.where(dest_ref[0, b] >= 0, wl_ref[0, b], 0)


def row_mask(dest_ref, wl_ref, step):
    i = lax.broadcasted_iota(jnp.int32, (TM, 1), 0)
    m = jnp.zeros((TM, 1), F32)
    for b in range(4):
        n = live_len(dest_ref, wl_ref, 4 * step + b)
        m = jnp.where((i >= 64 * b) & (i < 64 * b + n), 1.0, m)
    return m


def key_mask(dest_ref, wl_ref, pair):
    lane = lanes((1, 256))
    n0 = jnp.maximum(live_len(dest_ref, wl_ref, 2 * pair), 1)
    n1 = jnp.maximum(live_len(dest_ref, wl_ref, 2 * pair + 1), 1)
    n = jnp.where((lane // 64) % 2 == 0, n0, n1)
    return jnp.where(lane % 64 < n, 1.0, 0.0)


GAIN, BIAS, OS, OB, QS, QB = 0, 1, 2, 3, 4, 7


def forward_body(
    idx_ref, dest_ref, wl_ref, x_ref, dy_ref, vec_ref, w_ref,
    qkv_ref, p_ref, att_ref, gs_ref, ht_ref, attk_ref, send_ref,
    perm_ref, ones_ref, atts_ref, gsall_ref,
):
    step = pl.program_id(0)

    @pl.when(step == 0)
    def _():
        perm_ref[...] = row_order(idx_ref[0])
        ones_ref[...] = segment_ones()

    @pl.when(step < 4)
    def _():
        x = x_ref[...].astype(F32)
        cen = x - jnp.mean(x, axis=-1, keepdims=True)
        inv = lax.rsqrt(jnp.mean(cen * cen, axis=-1, keepdims=True) + 1e-06)
        hidden = (cen * inv * vec_ref[GAIN : GAIN + 1] + vec_ref[BIAS : BIAS + 1]).astype(BF)
        ht_ref[...] = nt(perm_ref[...], hidden).astype(BF)
        rm = row_mask(dest_ref, wl_ref, step)
        gs = (dy_ref[...].astype(F32) * rm * vec_ref[OS : OS + 1]).astype(BF)
        gs_ref[...] = gs
        row = pl.multiple_of(step * TM, TM)
        gsall_ref[pl.ds(row, TM), :] = gs
        for c in range(3):
            for h in range(2):
                lo = h * HALF
                cols = slice(c * D + lo, c * D + lo + HALF)
                acc = nn(hidden, w_ref[:, cols])
                qs = vec_ref[QS + c : QS + c + 1, lo : lo + HALF]
                qb = vec_ref[QB + c : QB + c + 1, lo : lo + HALF]
                qkv_ref[:, cols] = (acc * qs + qb).astype(BF)
        ones = ones_ref[...]
        for b in range(2):
            rows = slice(b * 128, (b + 1) * 128)
            km = key_mask(dest_ref, wl_ref, 2 * step + b)
            for g in range(2):
                outs = []
                for i in range(NHP):
                    in_a, in_b = head_masks(i)
                    lo = g * HALF + 128 * i
                    q = qkv_ref[rows, lo : lo + 256]
                    k = qkv_ref[rows, D + lo : D + lo + 256]
                    v = qkv_ref[rows, 2 * D + lo : 2 * D + lo + 256]
                    s = pack(nt(q, stack_heads(k, in_a, in_b)))
                    e = jnp.exp(s * SCALE) * km
                    p = e / segment_sum(e, ones)
                    p_ref[b, g * NHP + i] = p
                    outs.append(nn(unpack(p.astype(BF)), stack_heads(v, in_a, in_b)))
                att_ref[rows, g * HALF : (g + 1) * HALF] = join_windows(outs).astype(BF)
        turned = nt(perm_ref[...], att_ref[...]).astype(BF)
        attk_ref[...] = turned[:640]
        atts_ref[:, pl.ds(row, TM)] = turned[640:]

    @pl.when(step >= 4)
    def _():
        row = pl.multiple_of((step - 4) * 320, 320)
        send_ref[...] = nn(atts_ref[pl.ds(row, 320), :], gsall_ref[...]).astype(BF)


def whole(shape):
    return pl.BlockSpec(shape, lambda i: tuple(0 for _ in shape), pipeline_mode=pl.Buffered(1))


def smem():
    return pl.BlockSpec(memory_space=pltpu.SMEM)


def params():
    return pltpu.CompilerParams(
        dimension_semantics=("arbitrary",), vmem_limit_bytes=VMEM
    )


def cost(us):
    return pl.CostEstimate(
        flops=us * 8 * 10**8, transcendentals=0, bytes_accessed=us * 10**6
    )


def forward_call(idx, dest, wl, x, dy, vec, w):
    t = x.shape[0]
    tile = lambda i: jnp.minimum(i, 3)
    rows = lambda n: pl.BlockSpec((TM, n), lambda i: (tile(i), 0))
    return pl.pallas_call(
        forward_body,
        grid=(6,),
        in_specs=[
            smem(), smem(), smem(), rows(D), rows(D), whole((10, D)), whole((D, 3 * D)),
        ],
        out_specs=[
            rows(3 * D),
            pl.BlockSpec((2, 8, 64, 256), lambda i: (tile(i), 0, 0, 0)),
            rows(D), rows(D),
            pl.BlockSpec((D, TM), lambda i: (0, tile(i))),
            pl.BlockSpec((640, TM), lambda i: (0, tile(i))),
            pl.BlockSpec((320, D), lambda i: (jnp.maximum(i - 4, 0), 0)),
        ],
        out_shape=[
            jax.ShapeDtypeStruct((t, 3 * D), BF),
            jax.ShapeDtypeStruct((t // 128, 8, 64, 256), F32),
            jax.ShapeDtypeStruct((t, D), BF),
            jax.ShapeDtypeStruct((t, D), BF),
            jax.ShapeDtypeStruct((D, t), BF),
            jax.ShapeDtypeStruct((640, t), BF),
            jax.ShapeDtypeStruct((640, D), BF),
        ],
        scratch_shapes=[
            pltpu.VMEM((D, D), BF),
            pltpu.VMEM((256, 256), BF),
            pltpu.VMEM((640, t), BF),
            pltpu.VMEM((t, D), BF),
        ],
        compiler_params=params(),
        cost_estimate=cost(50),
        name="forward",
    )(idx, dest, wl, x, dy, vec, w)


def backward_body(
    q_ref, k_ref, v_ref, gs_ref, wo_ref, p_ref, vec_ref, ht_ref,
    gq_ref, gk_ref, gv_ref, send_ref, ga_ref, all_ref, ones_ref, *, half
):
    step = pl.program_id(0)

    @pl.when(step == 0)
    def _():
        ones_ref[...] = segment_ones()

    @pl.when(step < 4)
    def _():
        ga_ref[...] = nt(gs_ref[...], wo_ref[...]).astype(BF)
        ones = ones_ref[...]
        for b in range(2):
            rows = slice(b * 128, (b + 1) * 128)
            at = pl.multiple_of(step * TM + b * 128, 128)
            gqs, gks, gvs = [], [], []
            for i in range(NHP):
                in_a, in_b = head_masks(i)
                cols = slice(128 * i, 128 * i + 256)
                q, k = q_ref[rows, cols], k_ref[rows, cols]
                v, ga = v_ref[rows, cols], ga_ref[rows, cols]
                p = p_ref[b, i]
                gp = pack(nt(ga, stack_heads(v, in_a, in_b)))
                t = p * gp
                g = unpack((p * (gp - segment_sum(t, ones)) * SCALE).astype(BF))
                pf = unpack(p.astype(BF))
                gqs.append(nn(g, stack_heads(k, in_a, in_b)))
                gks.append(nn(pair_transpose(g), stack_heads(q, in_a, in_b)))
                gvs.append(nn(pair_transpose(pf), stack_heads(ga, in_a, in_b)))
            for n, (ws, o_ref) in enumerate(((gqs, gq_ref), (gks, gk_ref), (gvs, gv_ref))):
                qs = vec_ref[QS + n : QS + n + 1, half * HALF : (half + 1) * HALF]
                val = (join_windows(ws) * qs).astype(BF)
                o_ref[rows, :] = val
                all_ref[pl.ds(at, 128), n * HALF : (n + 1) * HALF] = val

    @pl.when(step >= 4)
    def _():
        row = pl.multiple_of((step - 4) * 320, 320)
        send_ref[...] = nn(ht_ref[pl.ds(row, 320), :], all_ref[...]).astype(BF)


def backward_call(half, qkv, gs, wo, p, vec, ht):
    t = gs.shape[0]
    tile = lambda i: jnp.minimum(i, 3)
    third = lambda n: pl.BlockSpec((TM, HALF), lambda i: (tile(i), 2 * n + half))
    part = pl.BlockSpec((TM, HALF), lambda i: (tile(i), 0))
    return pl.pallas_call(
        lambda *refs: backward_body(*refs, half=half),
        grid=(6,),
        in_specs=[
            third(0), third(1), third(2),
            pl.BlockSpec((TM, D), lambda i: (tile(i), 0)),
            pl.BlockSpec((HALF, D), lambda i: (half, 0), pipeline_mode=pl.Buffered(1)),
            pl.BlockSpec((2, NHP, 64, 256), lambda i: (tile(i), half, 0, 0)),
            whole((10, D)),
            pl.BlockSpec((640, t), lambda i: (1, 0), pipeline_mode=pl.Buffered(1)),
        ],
        out_specs=[
            part, part, part,
            pl.BlockSpec((320, 3 * HALF), lambda i: (jnp.maximum(i - 4, 0), 0)),
        ],
        out_shape=[jax.ShapeDtypeStruct((t, HALF), BF)] * 3
        + [jax.ShapeDtypeStruct((640, 3 * HALF), BF)],
        scratch_shapes=[
            pltpu.VMEM((TM, HALF), BF),
            pltpu.VMEM((t, 3 * HALF), BF),
            pltpu.VMEM((256, 256), BF),
        ],
        compiler_params=params(),
        cost_estimate=cost(25),
        name="backward%d" % half,
    )(qkv, qkv, qkv, gs, wo, p, vec, ht)


def keep_body(lhs_ref, got_ref, *refs, major):
    rhs, outs = refs[:-4], refs[-4:]
    step = pl.program_id(0)
    parts = []
    lo = 0
    for r in rhs:
        n = r.shape[1]
        acc = nn(lhs_ref[...], r[...]) + got_ref[:, lo : lo + n].astype(F32)
        parts.append((slice(lo, lo + n), acc.astype(BF)))
        lo += n
    for k in range(4):

        @pl.when(step == k)
        def _():
            for cols, val in parts:
                if major:
                    outs[k][:, cols] = val
                else:
                    for i in range(4):
                        outs[i][40 * k : 40 * k + 40, cols] = val[40 * i : 40 * i + 40]


def keep_call(name, lhs, got, rhs, major):
    t = lhs.shape[1]
    n = got.shape[1]
    out = pl.BlockSpec((160, n), lambda i: (0, 0))
    return pl.pallas_call(
        lambda *refs: keep_body(*refs, major=major),
        grid=(4,),
        in_specs=[
            pl.BlockSpec((160, t), lambda i: (i, 0)),
            pl.BlockSpec((160, n), lambda i: (i, 0)),
        ]
        + [whole(r.shape) for r in rhs],
        out_specs=[out] * 4,
        out_shape=[jax.ShapeDtypeStruct((160, n), BF)] * 4,
        compiler_params=params(),
        cost_estimate=cost(5),
        name=name,
    )(lhs, got, *rhs)


def embed_body(dest_ref, wl_ref, x_ref, att_ref, vec_ref, wo_ref, emb_ref):
    rm = row_mask(dest_ref, wl_ref, pl.program_id(0))
    out = nn(att_ref[...], wo_ref[...]) * vec_ref[OS : OS + 1] + vec_ref[OB : OB + 1]
    emb_ref[...] = ((out + x_ref[...].astype(F32)) * rm).astype(BF)


def embed_call(dest, wl, x, att, vec, wo):
    t = x.shape[0]
    rows = pl.BlockSpec((TM, D), lambda i: (i, 0))
    return pl.pallas_call(
        embed_body,
        grid=(t // TM,),
        in_specs=[smem(), smem(), rows, rows, whole((10, D)), whole((D, D))],
        out_specs=rows,
        out_shape=jax.ShapeDtypeStruct((t, D), BF),
        compiler_params=params(),
        cost_estimate=cost(8),
        name="embed",
    )(dest, wl, x, att, vec, wo)


def finish_body(
    dest_ref, wl_ref, x_ref, dy_ref, g0_ref, g1_ref, g2_ref, g3_ref, g4_ref, g5_ref,
    vec_ref, w_ref, pg_ref,
):
    rm = row_mask(dest_ref, wl_ref, pl.program_id(0))
    x = x_ref[...].astype(F32)
    cen = x - jnp.mean(x, axis=-1, keepdims=True)
    inv = lax.rsqrt(jnp.mean(cen * cen, axis=-1, keepdims=True) + 1e-06)
    normed = cen * inv
    gh = None
    for c, r in enumerate((g0_ref, g1_ref, g2_ref, g3_ref, g4_ref, g5_ref)):
        part = nt(r[...], w_ref[:, c * HALF : (c + 1) * HALF])
        gh = part if gh is None else gh + part
    gn = gh * vec_ref[GAIN : GAIN + 1]
    gl = inv * (
        gn
        - jnp.mean(gn, axis=-1, keepdims=True)
        - normed * jnp.mean(gn * normed, axis=-1, keepdims=True)
    )
    go = dy_ref[...].astype(F32) * rm
    pg_ref[...] = ((go + gl) * rm).astype(BF)


def finish_call(dest, wl, x, dy, parts, vec, w):
    t = x.shape[0]
    rows = lambda n: pl.BlockSpec((TM, n), lambda i: (i, 0))
    return pl.pallas_call(
        finish_body,
        grid=(t // TM,),
        in_specs=[smem(), smem(), rows(D), rows(D)]
        + [rows(HALF)] * 6
        + [whole((10, D)), whole((D, 3 * D))],
        out_specs=rows(D),
        out_shape=jax.ShapeDtypeStruct((t, D), BF),
        compiler_params=params(),
        cost_estimate=cost(20),
        name="finish",
    )(dest, wl, x, dy, *parts, vec, w)


def swap_cores(a):
    return lax.ppermute(a, "enc", [(i, i ^ 1) for i in range(8)])


def shift(a, axis, k):
    if axis == "x":
        perm = [(2 * x + c, 2 * ((x + k) % 4) + c) for x in range(4) for c in range(2)]
        return lax.ppermute(a, "enc", perm)
    if axis == "z":
        perm = [(4 * z + y, 4 * ((z + k) % 4) + y) for z in range(4) for y in range(4)]
    else:
        perm = [(4 * z + y, 4 * z + (y + k) % 4) for z in range(4) for y in range(4)]
    return lax.ppermute(a, "dp", perm)


def exchange(chunks, axis):
    return [shift(chunks[k], axis, k) for k in (2, 1, 3)]


def add_up(own, got):
    return sum((g.astype(F32) for g in got), own.astype(F32)).astype(BF)


def split(total, rows):
    return [total[k * rows : (k + 1) * rows] for k in range(4)]


def after(values, other):
    out = lax.optimization_barrier((values, other))
    return out[0]


def vectors(*rows):
    total = jnp.zeros((10 * D,), F32)
    lo = 0
    for r in rows:
        n = r.shape[0]
        total += lax.pad(r, jnp.float32(0), ((lo, 10 * D - lo - n, 0),))
        lo += n
    return total.reshape(10, D)


def local_work(idx, x, dy, dest, wl, gain, bias, w, qs, qb, wo, osc, ob, swap, exch):
    vec = vectors(gain, bias, osc, ob, qs, qb)
    qkv, p, att, gs, ht, attk, send_o = forward_call(idx, dest, wl, x, dy, vec, w)
    got_o = swap(send_o)
    gq0, gk0, gv0, send0 = backward_call(0, qkv, gs, wo, p, vec, ht)
    got_o = after(got_o, send0)
    got0 = swap(send0)
    own_o = keep_call("keep_o", attk, got_o, [gs], True)
    in_o = exch(own_o, "z")
    gq1, gk1, gv1, send1 = backward_call(1, after(qkv, own_o[0]), gs, wo, p, vec, ht)
    got0 = after(got0, send1)
    got1 = swap(send1)
    own_0 = keep_call("keep_0", ht, got0, [gq0, gk0, gv0], True)
    in_0 = exch(own_0, "z")
    got1 = after(got1, own_0[0])
    own_1 = keep_call("keep_1", ht, got1, [gq1, gk1, gv1], False)
    in_1 = exch(own_1, "y")
    in_o = after(in_o, own_1[0])
    sum_o = split(add_up(own_o[0], in_o), 40)
    in_o = exch(sum_o, "y")
    gq1 = after(gq1, (own_1[0], sum_o))
    pg = finish_call(dest, wl, x, dy, (gq0, gq1, gk0, gk1, gv0, gv1), vec, w)
    in_o, in_0, in_1 = after((in_o, in_0, in_1), pg)
    sum_0 = split(add_up(own_0[0], in_0), 40)
    sum_1 = split(add_up(own_1[0], in_1), 40)
    in_0 = exch(sum_0, "y")
    in_1 = exch(sum_1, "z")
    emb = embed_call(dest, wl, x, after(att, (sum_0, sum_1)), vec, wo)
    in_o, in_0, in_1 = after((in_o, in_0, in_1), emb)
    last = split(
        jnp.concatenate(
            [add_up(sum_o[0], in_o), add_up(sum_0[0], in_0), add_up(sum_1[0], in_1)], axis=1
        ),
        10,
    )
    in_x = exch(last, "x")
    return emb, pg, sum((g.astype(F32) for g in in_x), last[0].astype(F32))


def per_device(x, dy, dest, wl, gain, bias, w, qs, qb, wo, osc, ob):
    idx = (lax.axis_index("enc") * 16 + lax.axis_index("dp")).reshape(1).astype(jnp.int32)
    shape = x.shape
    emb, pg, mine = local_work(
        idx, x.reshape(-1, D), dy.reshape(-1, D), dest, wl,
        gain, bias, w, qs, qb, wo, osc, ob, swap_cores, exchange,
    )
    qkv_grad = jnp.zeros((10, 3 * D), F32)
    for c in range(3):
        for h in range(2):
            part = mine[:, D + (3 * h + c) * HALF :][:, :HALF]
            lo = (2 * c + h) * HALF
            qkv_grad += lax.pad(
                part, jnp.float32(0), ((0, 0, 0), (lo, 3 * D - HALF - lo, 0))
            )
    return emb.reshape(shape), pg.reshape(shape), qkv_grad, mine[:, :D]


def solution(mesh):
    big = P("dp", "enc", None, None)
    small = P("dp", "enc")
    return jax.shard_map(
        per_device,
        mesh=mesh,
        in_specs=(big, big, small, small) + (P(),) * 8,
        out_specs=(big, big, P(("enc", "dp"), None), P(("enc", "dp"), None)),
        check_vma=False,
    )
```
